512 devices in a mesh: leaf: 32 (over y, x, core), col: 16 (over z).
Axes of the slice: x: 4, y: 4, z: 16, core: 2. Of those that a mesh axis runs over, the one named last changes fastest.
Arguments:
- histograms: bfloat16 [4, 128, 1024, 512], P(None, 'leaf', 'col'), may hold values from -6 to 6
- diag_inv: bfloat16 [4, 128, 512, 512], P(None, 'leaf', 'col'), as said below
- below_panel: bfloat16 [4, 128, 256, 512], P(None, 'leaf', 'col'), may hold values from -0.1875 to 0.1875
- parent_map: int32 [3, 128], P(None, 'leaf'), may hold values from 0 to 127, as said below
- row_lists: int32 [3, 128, 256], P(None, 'leaf'), may hold values from 0 to 511, as said below
Outputs:
- solution: bfloat16 [4, 128, 1024, 512], P(None, 'leaf', 'col')
- upward: bfloat16 [128, 1024, 256], P('leaf', 'col')
The draws below stay inside these ranges and needn't reach their ends.
Inputs may be any that keep to these rules, and one draw needn't show every extreme that they name: `parent_map`: entry [l, j] names a supernode of tier l + 1 whose owner (index // 4) is the owner of supernode j (j // 4) or the leaf index that differs from it in bit l mod log2(32); at every tier some leaf index sends all its updates to that other index. `row_lists`: the 256 entries of each list are distinct. `diag_inv`: every block is lower triangular with a positive diagonal.
All inputs are finite; a program needn't handle non-finite values.
Results may differ from the reference program's by a relative error of at most 0.012.
Values may be sent and summed in bfloat16 or wider, within the bound.
A program may use at most 64 MiB of HBM per device.

```python
import math
import jax
import jax.numpy as jnp
from jax import lax

W = 512
R = 256
COLS = 1024
LEVELS = 4
SN_DEV = 4
NS = 128
N_LEAF = 32


def draw_diag_inv(key, part):
    key_lower, key_pivot = jax.random.split(key)
    below_diag = jax.random.normal(key_lower, (LEVELS, NS, W, W), jnp.float32) * (0.8 / math.sqrt(W))
    pivots = jax.random.uniform(key_pivot, (LEVELS, NS, W), jnp.float32, 0.6, 1.2)
    positions = jnp.arange(W)
    strictly = (positions[:, None] > positions[None, :]).astype(jnp.float32)
    identity = (positions[:, None] == positions[None, :]).astype(jnp.float32)
    return (below_diag * strictly + pivots[..., None] * identity).astype(jnp.bfloat16)


def draw_parent_map(key, part):
    key_tend, key_roll, key_force, key_slot = jax.random.split(key, 4)
    bit_count = max(N_LEAF.bit_length() - 1, 1)
    children = jnp.arange(NS, dtype=jnp.int32)
    owners = children // SN_DEV
    tiers = jnp.arange(LEVELS - 1, dtype=jnp.int32)
    tendency = jax.random.randint(key_tend, (LEVELS - 1, N_LEAF), 0, 5)
    rolled = jax.random.randint(key_roll, (LEVELS - 1, NS), 0, 4)
    leaving = rolled < tendency[:, owners]
    forced = jax.random.randint(key_force, (LEVELS - 1, 1), 0, N_LEAF)
    leaving = jnp.logical_or(leaving, owners[None, :] == forced)
    partner_bit = jnp.left_shift(jnp.ones_like(tiers), tiers % bit_count)[:, None]
    partner = jnp.bitwise_xor(owners[None, :], partner_bit)
    target = jnp.where(leaving, partner, owners[None, :])
    slots = jax.random.randint(key_slot, (LEVELS - 1, NS), 0, SN_DEV)
    return (target * SN_DEV + slots).astype(jnp.int32)


def draw_row_lists(key, part):
    key_list = jax.random.split(key, (LEVELS - 1) * NS)
    orders = jax.vmap(lambda single: jax.random.permutation(single, W)[:R])(key_list)
    return orders.reshape(LEVELS - 1, NS, R).astype(jnp.int32)


def steps_of(key, shape, shards, smallest, high):
    level = 1.0
    for position, blocks in shards:
        draws = jax.random.uniform(jax.random.fold_in(jax.random.fold_in(key, 6), position), (blocks,), jnp.float32, smallest / len(shards), high / len(shards))
        level = level * jnp.repeat(jnp.exp(draws), shape[position] // blocks).reshape((-1,) + (1,) * (len(shape) - 1 - position))
    return level


def bell_draw(rng, dims, spread, limit, cuts=(), kind=jnp.bfloat16):
    entries = jax.random.normal(rng, dims, jnp.float32) * spread
    if len(cuts) > 0:
        entries = steps_of(rng, dims, cuts, -0.22, 0.18) * entries
    return jnp.clip(entries, min=-limit, max=limit).astype(kind)


def setup_inputs(seed: int = 0) -> dict:
    seeds = jax.random.split(jax.random.key(seed), 6)
    histograms = bell_draw(seeds[0], (LEVELS, NS, COLS, W), 1.0, 6.0, ((1, 32), (2, 16)))
    diag_inv = draw_diag_inv(jax.random.fold_in(seeds[5], 71), 0)
    below_panel = bell_draw(seeds[2], (LEVELS, NS, R, W), (2 * W) ** -0.5, 0.1875, ((1, 32), (2, 16)))
    parent_map = draw_parent_map(jax.random.fold_in(seeds[5], 71), 0)
    row_lists = draw_row_lists(jax.random.fold_in(seeds[5], 71), 0)
    return {"histograms": histograms, "diag_inv": diag_inv, "below_panel": below_panel, "parent_map": parent_map, "row_lists": row_lists}


def reference(histograms, diag_inv, below_panel, parent_map, row_lists):
    incoming = jnp.zeros((NS, COLS, W), jnp.float32)
    columns = jnp.arange(COLS, dtype=jnp.int32)
    solved = []
    upward = jnp.zeros((NS, COLS, R), jnp.bfloat16)
    for height in range(LEVELS):
        source = (histograms[height].astype(jnp.float32) - incoming).astype(jnp.bfloat16)
        source = lax.optimization_barrier(source)
        result = jnp.einsum("scw,svw->scv", source.astype(jnp.float32), diag_inv[height].astype(jnp.float32))
        answer = result.astype(jnp.bfloat16)
        answer = lax.optimization_barrier(answer)
        solved.append(answer)
        update = jnp.einsum("scw,srw->scr", answer.astype(jnp.float32), below_panel[height].astype(jnp.float32))
        if height == LEVELS - 1:
            upward = update.astype(jnp.bfloat16)
        else:
            targets = parent_map[height].astype(jnp.int32)
            lists = row_lists[height].astype(jnp.int32)
            incoming = jnp.zeros((NS, COLS, W), jnp.float32).at[targets[:, None, None], columns[None, :, None], lists[:, None, :]].add(update)
    return jnp.stack(solved), upward
```

```python
import functools
import jax
import jax.numpy as jnp
from jax import lax
from jax.experimental import pallas as pl
from jax.experimental.pallas import tpu as pltpu
from jax.sharding import PartitionSpec as P

MESH = pl.DeviceIdType.MESH
F32, BF16 = jnp.float32, jnp.bfloat16

RING = 16
TIERS = 4
SLOTS = 4
COLS = 64
WIDTH = 512
ROWS = 256
PIECE = 32
DEPTH = 16
LANES = 128
NARROW = 32

UP_DIAG = (9, 8, 7, 6, 9, 6, 6, 7, 6, 6, 6, 7, 7, 9, 9, 9)
UP_BELOW = (9, 9, 9, 9, 7, 6, 7, 6, 6, 6, 7, 9, 9, 8, 6, 9)
MAX_HOP = 9
PERIOD = 6
SHIFT = 3
LAG = 3
LAST = (TIERS - 1) * PERIOD + SHIFT + MAX_HOP
NT = (((1,), (1,)), ((), ()))


def table(values):
    low = sum((v - 6) << (2 * i) for i, v in enumerate(values[:8]))
    high = sum((v - 6) << (2 * i) for i, v in enumerate(values[8:]))
    return low, high


def hops_up(words, z):
    word = jnp.where(z < 8, jnp.int32(words[0]), jnp.int32(words[1]))
    return 6 + lax.rem(lax.shift_right_logical(word, 2 * lax.rem(z, 8)), 4)


def by_width(z, act, low=0, high=RING):
    if high - low == 1:
        act(high)
        return
    middle = (low + high) // 2

    def lower():
        by_width(z, act, low, middle)

    def upper():
        by_width(z, act, middle, high)

    lax.cond(z < middle, lower, upper)


def kernel(
    hist_hbm, diag_hbm, below_hbm, parent_ref, rows_ref,
    solved_hbm, upward_hbm,
    hist, diag, gathered, panels, spread, answer, kept, leaving, outbox, inbox, top,
    load_sem, diag_send, diag_recv, below_send, below_recv, swap_send, swap_recv, store_sem,
):
    me = lax.axis_index("col")
    leaf = lax.axis_index("leaf")
    above = lax.rem(me + 1, RING)
    under = lax.rem(me + RING - 1, RING)
    ups = table(UP_DIAG), table(UP_BELOW)

    def partner(bit):
        return leaf + (1 << bit) * (1 - 2 * lax.rem(leaf // (1 << bit), 2))

    loads = [
        pltpu.make_async_copy(diag_hbm.at[0], diag.at[0], load_sem.at[0]),
        pltpu.make_async_copy(below_hbm.at[0], panels.at[0, me], load_sem.at[1]),
    ]
    for t in range(1, TIERS):
        loads.append(pltpu.make_async_copy(diag_hbm.at[t], diag.at[t], load_sem.at[2 * t]))
        loads.append(pltpu.make_async_copy(below_hbm.at[t], panels.at[t, me], load_sem.at[2 * t + 1]))
    loads.append(pltpu.make_async_copy(hist_hbm, hist, load_sem.at[2 * TIERS]))
    for load in loads:
        load.start()

    barrier = pltpu.get_barrier_semaphore()
    for ring in (above, under):
        pl.semaphore_signal(barrier, inc=1, device_id={"col": ring}, device_id_type=MESH)
    for bit in range(TIERS - 1):
        pl.semaphore_signal(barrier, inc=1, device_id={"leaf": partner(bit)}, device_id_type=MESH)

    group = lax.broadcasted_iota(jnp.int32, (1, LANES), 1) // NARROW

    def pack(t):
        loads[2 * t].wait()
        loads[2 * t + 1].wait()
        for q in range(WIDTH // LANES):
            wide = [diag[t, s, :, q * LANES:(q + 1) * LANES].astype(F32) for s in range(SLOTS)]
            for a in range(LANES // NARROW):
                tile = jnp.zeros((PIECE, LANES), F32)
                for s in range(SLOTS):
                    turn = NARROW * ((s - a) % 4)
                    moved = pltpu.roll(wide[s], turn, axis=1) if turn else wide[s]
                    tile = jnp.where(group == s, moved, tile)
                gathered[t, me, 4 * q + a] = tile.astype(BF16)

    def gather_diag(direction, t, k):
        z = lax.rem(me - k + RING, RING) if direction == 0 else lax.rem(me + k, RING)
        far = hops_up(ups[0], z)
        if direction:
            far = RING - 1 - far
        target = above if direction == 0 else under

        def act(n):
            block = gathered.at[t, z, pl.ds(0, n)]
            copy = pltpu.make_async_remote_copy(
                src_ref=block, dst_ref=block,
                send_sem=diag_send.at[direction, t, k], recv_sem=diag_recv.at[direction, t, k],
                device_id={"col": target}, device_id_type=MESH,
            )
            arriving = pltpu.make_async_remote_copy(
                src_ref=block, dst_ref=block,
                send_sem=diag_send.at[direction, t, k],
                recv_sem=diag_recv.at[direction, t, jnp.maximum(k - 1, 0)],
                device_id={"col": target}, device_id_type=MESH,
            )

            @pl.when(k >= 1)
            def _():
                arriving.wait_recv()

            @pl.when(k < far)
            def _():
                copy.start()

        @pl.when(k <= far)
        def _():
            by_width(z, act)

    def drain_diag(direction, t, k):
        z = lax.rem(me - k + RING, RING) if direction == 0 else lax.rem(me + k, RING)
        far = hops_up(ups[0], z)
        if direction:
            far = RING - 1 - far
        target = above if direction == 0 else under

        def act(n):
            block = gathered.at[t, z, pl.ds(0, n)]
            pltpu.make_async_remote_copy(
                src_ref=block, dst_ref=block,
                send_sem=diag_send.at[direction, t, k], recv_sem=diag_recv.at[direction, t, k],
                device_id={"col": target}, device_id_type=MESH,
            ).wait_send()

        @pl.when(k < far)
        def _():
            by_width(z, act)

    def below_copy(direction, t, k, landed, z):
        block = panels.at[t, z]
        return pltpu.make_async_remote_copy(
            src_ref=block, dst_ref=block,
            send_sem=below_send.at[direction, t, k], recv_sem=below_recv.at[direction, t, landed],
            device_id={"col": above if direction == 0 else under}, device_id_type=MESH,
        )

    def gather_below(direction, t, k):
        z = lax.rem(me - k + RING, RING) if direction == 0 else lax.rem(me + k, RING)
        far = hops_up(ups[1], z)
        if direction:
            far = RING - 1 - far

        @pl.when(jnp.logical_and(k >= 1, k <= far))
        def _():
            below_copy(direction, t, k, jnp.maximum(k - 1, 0), z).wait_recv()

        @pl.when(k < far)
        def _():
            below_copy(direction, t, k, k, z).start()

    def drain_below(direction, t, k):
        z = lax.rem(me - k + RING, RING) if direction == 0 else lax.rem(me + k, RING)
        far = hops_up(ups[1], z)
        if direction:
            far = RING - 1 - far

        @pl.when(k < far)
        def _():
            below_copy(direction, t, k, k, z).wait_send()

    def swap(t):
        return pltpu.make_async_remote_copy(
            src_ref=outbox.at[t], dst_ref=inbox.at[t],
            send_sem=swap_send.at[t], recv_sem=swap_recv.at[t],
            device_id={"leaf": partner(t)}, device_id_type=MESH,
        )

    def store(t):
        return pltpu.make_async_copy(answer.at[t], solved_hbm.at[t], store_sem.at[t])

    def make_source(t):
        if t == 0:
            loads[2 * TIERS].wait()
        else:
            swap(t - 1).wait()
        for s in range(SLOTS):
            values = hist[t, s].astype(F32)
            if t > 0:
                values = values - (kept[s] + inbox[t - 1, s].astype(F32))
            values = values.astype(BF16).astype(F32)
            for m in range(WIDTH // NARROW):
                q, a = m // 4, m % 4
                tile = values[:, q * LANES:(q + 1) * LANES]
                turn = NARROW * ((s - a) % 4)
                if turn:
                    tile = pltpu.roll(tile, turn, axis=1)
                tile = jnp.where(group == s, tile, 0.0).astype(BF16)
                spread[s * COLS:(s + 1) * COLS, m * LANES:(m + 1) * LANES] = tile

    def solve(t, half):
        tiles = 8 if half == 0 else 16
        columns = []
        for m in range(tiles):
            blocks = []
            for z in range(8 * half, 8 * half + 8):
                blocks.append(gathered[t, z, m] if z >= m else jnp.zeros((PIECE, LANES), BF16))
            columns.append(jnp.concatenate(blocks, axis=0))
        weights = jnp.concatenate(columns, axis=1)
        result = lax.dot_general(spread[:, :tiles * LANES], weights, NT, preferred_element_type=F32)
        result = result.astype(BF16)
        for s in range(SLOTS):
            answer[t, s, :, half * 256:(half + 1) * 256] = result[s * COLS:(s + 1) * COLS]

    def updated(t, s):
        panel = jnp.concatenate([panels[t, z, s] for z in range(RING)], axis=0)
        return lax.dot_general(answer[t, s], panel, NT, preferred_element_type=F32)

    def place(t, s):
        update = updated(t, s)
        upper = update.astype(BF16)
        lower = (update - upper.astype(F32)).astype(BF16)
        both = jnp.concatenate([upper, lower], axis=0)
        wanted = rows_ref[t, s:s + 1, :]
        landing = lax.broadcasted_iota(jnp.int32, (WIDTH, ROWS), 0) == wanted
        landing = landing.astype(F32).astype(BF16)
        placed = lax.dot_general(both, landing, NT, preferred_element_type=F32)
        placed = placed[:COLS] + placed[COLS:]
        parent = parent_ref[t, s]
        owner = parent // SLOTS
        slot = lax.rem(parent, SLOTS)
        stays = owner == leaf
        for p in range(SLOTS):
            here = jnp.where(jnp.logical_and(stays, slot == p), placed, 0.0)
            there = jnp.where(jnp.logical_and(jnp.logical_not(stays), slot == p), placed, 0.0)
            if s == 0:
                kept[p] = here
                leaving[p] = there
            else:
                kept[p] += here
                leaving[p] += there
        if s == SLOTS - 1:
            outbox[t] = leaving[...].astype(BF16)

    pack(0)
    pl.semaphore_wait(barrier, 2 + TIERS - 1)

    plan = {}

    def at(slot, unit):
        plan.setdefault(slot, []).append(unit)

    for t in range(1, TIERS):
        at(t - 1, functools.partial(pack, t))
    for t in range(TIERS):
        ready = t * PERIOD + MAX_HOP + (1 if t else 0)

        def first(t=t):
            make_source(t)
            solve(t, 0)

        def second(t=t):
            solve(t, 1)
            store(t).start()

        at(ready, first)
        at(ready + 1, second)
        whole = t * PERIOD + SHIFT + MAX_HOP
        if t < TIERS - 1:
            for s in range(2):
                at(whole, functools.partial(place, t, s))
            for s in range(2, 4):
                at(whole + 1, functools.partial(place, t, s))
            at(whole + 2, lambda t=t: swap(t).start())

    def step(slot, carry):
        for ago in (1, 0):
            t = slot // PERIOD - ago
            k = slot - PERIOD * t
            for direction in range(2):
                @pl.when(jnp.logical_and(jnp.logical_and(t >= 0, t < TIERS), k <= MAX_HOP))
                def _():
                    gather_diag(direction, t, k)

            @pl.when(jnp.logical_and(jnp.logical_and(t >= 0, t < TIERS), jnp.logical_and(k >= LAG, k < LAG + MAX_HOP)))
            def _():
                for direction in range(2):
                    drain_diag(direction, t, k - LAG)
        for ago in (1, 0):
            later = slot - SHIFT + PERIOD
            t = later // PERIOD - 1 - ago
            k = later - PERIOD * (t + 1)
            for direction in range(2):
                @pl.when(jnp.logical_and(jnp.logical_and(t >= 0, t < TIERS), k <= MAX_HOP))
                def _():
                    gather_below(direction, t, k)

            @pl.when(jnp.logical_and(jnp.logical_and(t >= 0, t < TIERS), jnp.logical_and(k >= LAG, k < LAG + MAX_HOP)))
            def _():
                for direction in range(2):
                    drain_below(direction, t, k - LAG)
        for when, units in plan.items():
            @pl.when(slot == when)
            def _():
                for unit in units:
                    unit()
        return carry

    lax.fori_loop(0, LAST + 1, step, 0)
    for s in range(SLOTS):
        top[s] = updated(TIERS - 1, s).astype(BF16)
    last = pltpu.make_async_copy(top, upward_hbm, store_sem.at[TIERS])
    last.start()

    def finish(slot, carry):
        for ago in (1, 0):
            later = slot - SHIFT + PERIOD
            t = later // PERIOD - 1 - ago
            k = later - PERIOD * (t + 1)

            @pl.when(jnp.logical_and(jnp.logical_and(t >= 0, t < TIERS), jnp.logical_and(k >= LAG, k < LAG + MAX_HOP)))
            def _():
                for direction in range(2):
                    drain_below(direction, t, k - LAG)
        return carry

    lax.fori_loop(LAST + 1, LAST + LAG, finish, 0)
    for t in range(TIERS):
        store(t).wait()
    last.wait()


def on_device(histograms, diag_inv, below_panel, parent_map, row_lists):
    vmem = pltpu.VMEM
    dma = pltpu.SemaphoreType.DMA
    return pl.pallas_call(
        kernel,
        out_shape=(
            jax.ShapeDtypeStruct((TIERS, SLOTS, COLS, WIDTH), BF16),
            jax.ShapeDtypeStruct((SLOTS, COLS, ROWS), BF16),
        ),
        in_specs=[
            pl.BlockSpec(memory_space=pl.ANY),
            pl.BlockSpec(memory_space=pl.ANY),
            pl.BlockSpec(memory_space=pl.ANY),
            pl.BlockSpec(memory_space=pltpu.SMEM),
            pl.BlockSpec(memory_space=pltpu.VMEM),
        ],
        out_specs=(pl.BlockSpec(memory_space=pl.ANY), pl.BlockSpec(memory_space=pl.ANY)),
        scratch_shapes=[
            vmem((TIERS, SLOTS, COLS, WIDTH), BF16),
            vmem((TIERS, SLOTS, PIECE, WIDTH), BF16),
            vmem((TIERS, RING, RING, PIECE, LANES), BF16),
            vmem((TIERS, RING, SLOTS, DEPTH, WIDTH), BF16),
            vmem((SLOTS * COLS, RING * LANES), BF16),
            vmem((TIERS, SLOTS, COLS, WIDTH), BF16),
            vmem((SLOTS, COLS, WIDTH), F32),
            vmem((SLOTS, COLS, WIDTH), F32),
            vmem((TIERS - 1, SLOTS, COLS, WIDTH), BF16),
            vmem((TIERS - 1, SLOTS, COLS, WIDTH), BF16),
            vmem((SLOTS, COLS, ROWS), BF16),
            dma((2 * TIERS + 1,)),
            dma((2, TIERS, MAX_HOP + 1)),
            dma((2, TIERS, MAX_HOP + 1)),
            dma((2, TIERS, MAX_HOP + 1)),
            dma((2, TIERS, MAX_HOP + 1)),
            dma((TIERS - 1,)),
            dma((TIERS - 1,)),
            dma((TIERS + 1,)),
        ],
        compiler_params=pltpu.CompilerParams(
            collective_id=0, has_side_effects=True, vmem_limit_bytes=60 << 20
        ),
    )(histograms, diag_inv, below_panel, parent_map, row_lists)


def solution(mesh):
    return jax.shard_map(
        on_device,
        mesh=mesh,
        in_specs=(
            P(None, "leaf", "col", None),
            P(None, "leaf", "col", None),
            P(None, "leaf", "col", None),
            P(None, "leaf"),
            P(None, "leaf", None),
        ),
        out_specs=(P(None, "leaf", "col", None), P("leaf", "col", None)),
        check_vma=False,
    )
```

```python
import functools
import jax
import jax.numpy as jnp
from jax import lax
from jax.experimental import pallas as pl
from jax.experimental.pallas import tpu as pltpu
from jax.sharding import PartitionSpec as P

MESH = pl.DeviceIdType.MESH
F32, BF16 = jnp.float32, jnp.bfloat16

RING = 16
TIERS = 4
SLOTS = 4
COLS = 64
WIDTH = 512
ROWS = 256
PIECE = 32
DEPTH = 16
LANES = 128
NARROW = 32

HOPS_UP = (
    (9, 8, 6, 7, 7, 6, 6, 7, 6, 6, 7, 9, 9, 6, 9, 9),
    (9, 8, 10, 9, 6, 5, 8, 9, 7, 7, 8, 8, 8, 7, 8, 8),
    (10, 10, 10, 6, 9, 8, 6, 6, 6, 6, 5, 5, 10, 8, 10, 10),
)
PIECES = (
    (0, 0, 0),
    (1, 2, 0),
    (0, 1, 1),
    (2, 1, 7),
    (3, 2, 10),
    (3, 1, 11),
    (2, 2, 5),
    (1, 1, 4),
    (0, 2, 0),
    (3, 0, 9),
    (2, 0, 5),
    (1, 0, 2),
)
MAX_HOP = 10
REACH = tuple(
    max(max(r, 15 - r) for r in (up[8:] if piece == 1 else up)) for piece, up in enumerate(HOPS_UP)
)
LAG = 6
LAST = max(start + REACH[piece] for _, piece, start in PIECES)
HALF = RING // 2
SWAP_SLOTS = (1, 2, 2)
NT = (((1,), (1,)), ((), ()))


def table(values):
    low = sum((v - 5) << (3 * i) for i, v in enumerate(values[:8]))
    high = sum((v - 5) << (3 * i) for i, v in enumerate(values[8:]))
    return low, high


def hops_up(words, z):
    word = jnp.where(z < 8, jnp.int32(words[0]), jnp.int32(words[1]))
    return 5 + lax.rem(lax.shift_right_logical(word, 3 * lax.rem(z, 8)), 8)


def by_width(w, act, low=0, high=HALF):
    if high - low == 1:
        act(high)
        return
    middle = (low + high) // 2

    def lower():
        by_width(w, act, low, middle)

    def upper():
        by_width(w, act, middle, high)

    lax.cond(w < middle, lower, upper)


def kernel(
    hist_hbm, diag_hbm, below_hbm, parent_ref, rows_ref,
    solved_hbm, upward_hbm,
    hist, diag, gathered, panels, spread, answer, kept, placed, partial, lower, marks, guest_marks, card, guest, sorted_in, outbox, inbox, top,
    load_sem, ring_send, ring_recv, swap_send, swap_recv, card_send, card_recv, store_sem,
):
    me = lax.axis_index("col")
    leaf = lax.axis_index("leaf")
    above = lax.rem(me + 1, RING)
    under = lax.rem(me + RING - 1, RING)
    ups = [table(values) for values in HOPS_UP]

    def partner(bit):
        return leaf + (1 << bit) * (1 - 2 * lax.rem(leaf // (1 << bit), 2))

    loads = [
        pltpu.make_async_copy(diag_hbm.at[0], diag.at[0], load_sem.at[0]),
        pltpu.make_async_copy(below_hbm.at[0], panels.at[0, me], load_sem.at[1]),
    ]
    for t in range(1, TIERS):
        loads.append(pltpu.make_async_copy(diag_hbm.at[t], diag.at[t], load_sem.at[2 * t]))
        loads.append(pltpu.make_async_copy(below_hbm.at[t], panels.at[t, me], load_sem.at[2 * t + 1]))
    loads.append(pltpu.make_async_copy(hist_hbm, hist, load_sem.at[2 * TIERS]))
    for load in loads:
        load.start()

    barrier = pltpu.get_barrier_semaphore()
    for ring in (above, under):
        pl.semaphore_signal(barrier, inc=1, device_id={"col": ring}, device_id_type=MESH)
    for bit in range(TIERS - 1):
        pl.semaphore_signal(barrier, inc=1, device_id={"leaf": partner(bit)}, device_id_type=MESH)

    group = lax.broadcasted_iota(jnp.int32, (1, LANES), 1) // NARROW

    def pack(t):
        loads[2 * t].wait()
        for q in range(WIDTH // LANES):
            wide = [diag[t, s, :, q * LANES:(q + 1) * LANES].astype(F32) for s in range(SLOTS)]
            for a in range(LANES // NARROW):
                tile = jnp.zeros((PIECE, LANES), F32)
                for s in range(SLOTS):
                    turn = NARROW * ((s - a) % 4)
                    moved = pltpu.roll(wide[s], turn, axis=1) if turn else wide[s]
                    tile = jnp.where(group == s, moved, tile)
                gathered[t, me, 4 * q + a] = tile.astype(BF16)

    def aim(direction, piece, k):
        z = lax.rem(me - k + RING, RING) if direction == 0 else lax.rem(me + k, RING)
        far = hops_up(ups[piece], z)
        if direction:
            far = RING - 1 - far
        if piece == 1:
            far = jnp.where(z >= HALF, far, -1)
        return z, far

    def each_block(piece, t, z, act):
        if piece == 2:
            act(panels.at[t, z])
        elif piece == 1:
            by_width(z - HALF, lambda n: act(gathered.at[t, z, pl.ds(HALF, n)]))
        else:
            by_width(jnp.minimum(z, HALF - 1), lambda n: act(gathered.at[t, z, pl.ds(0, n)]))

    def ring_copy(direction, piece, t, block, k, landed):
        return pltpu.make_async_remote_copy(
            src_ref=block, dst_ref=block,
            send_sem=ring_send.at[direction, piece, t, k],
            recv_sem=ring_recv.at[direction, piece, t, landed],
            device_id={"col": above if direction == 0 else under}, device_id_type=MESH,
        )

    def gather(direction, piece, t, k):
        z, far = aim(direction, piece, k)

        def act(block):
            @pl.when(k >= 1)
            def _():
                ring_copy(direction, piece, t, block, k, jnp.maximum(k - 1, 0)).wait_recv()

            @pl.when(k < far)
            def _():
                ring_copy(direction, piece, t, block, k, k).start()

        @pl.when(k <= far)
        def _():
            each_block(piece, t, z, act)

    def drain(direction, piece, t, k):
        z, far = aim(direction, piece, k)

        @pl.when(k < far)
        def _():
            each_block(piece, t, z, lambda block: ring_copy(direction, piece, t, block, k, k).wait_send())

    def swap(t):
        return pltpu.make_async_remote_copy(
            src_ref=outbox.at[t], dst_ref=inbox.at[t],
            send_sem=swap_send.at[t], recv_sem=swap_recv.at[t],
            device_id={"leaf": partner(t)}, device_id_type=MESH,
        )

    def store(t):
        return pltpu.make_async_copy(answer.at[t], solved_hbm.at[t], store_sem.at[t])

    def make_source(t, s):
        if s == 0:
            if t == 0:
                loads[2 * TIERS].wait()
        values = hist[t, s].astype(F32)
        if t > 0:
            values = values - kept[s]
        values = values.astype(BF16).astype(F32)
        for m in range(WIDTH // NARROW):
            q, a = m // 4, m % 4
            tile = values[:, q * LANES:(q + 1) * LANES]
            turn = NARROW * ((s - a) % 4)
            if turn:
                tile = pltpu.roll(tile, turn, axis=1)
            tile = jnp.where(group == s, tile, 0.0).astype(BF16)
            spread[s * COLS:(s + 1) * COLS, m * LANES:(m + 1) * LANES] = tile

    def solve(t, half, part):
        columns = []
        for m in range(HALF * part, HALF * part + HALF):
            blocks = []
            for z in range(HALF * half, HALF * half + HALF):
                blocks.append(gathered[t, z, m] if z >= m else jnp.zeros((PIECE, LANES), BF16))
            columns.append(jnp.concatenate(blocks, axis=0))
        weights = jnp.concatenate(columns, axis=1)
        result = lax.dot_general(
            spread[:, HALF * LANES * part:HALF * LANES * (part + 1)], weights, NT, preferred_element_type=F32
        )
        if half == 1 and part == 0:
            partial[...] = result
            return
        if half == 1:
            result = partial[...] + result
        result = result.astype(BF16)
        for s in range(SLOTS):
            answer[t, s, :, half * 256:(half + 1) * 256] = result[s * COLS:(s + 1) * COLS]
        if half == 1:
            store(t).start()

    def updated(t, s):
        panel = jnp.concatenate([panels[t, z, s] for z in range(RING)], axis=0)
        return lax.dot_general(answer[t, s], panel, NT, preferred_element_type=F32)

    def mark(source, marks, t, s):
        hit = lax.broadcasted_iota(jnp.int32, (WIDTH, ROWS), 0) == source[t, s:s + 1, :ROWS]
        marks[t, :, s * ROWS:(s + 1) * ROWS] = hit.astype(F32).astype(BF16)

    def describe(t):
        card[t, :, :ROWS] = rows_ref[t]
        for s in range(SLOTS):
            card[t, s:s + 1, ROWS:] = jnp.full((1, ROWS), parent_ref[t, s], jnp.int32)

    def introduce(t):
        return pltpu.make_async_remote_copy(
            src_ref=card.at[t], dst_ref=guest.at[t],
            send_sem=card_send.at[t], recv_sem=card_recv.at[t],
            device_id={"leaf": partner(t)}, device_id_type=MESH,
        )

    def update(t, s):
        value = updated(t, s)
        upper = value.astype(BF16)
        outbox[t, s] = upper
        lower[s] = (value - upper.astype(F32)).astype(BF16)

    def place(t, s):
        both = jnp.concatenate([outbox[t, s], lower[s]], axis=0)
        result = lax.dot_general(both, marks[t, :, s * ROWS:(s + 1) * ROWS], NT, preferred_element_type=F32)
        placed[s] = result[:COLS] + result[COLS:]

    def collect(t, p):
        total = jnp.zeros((COLS, WIDTH), F32)
        for s in range(SLOTS):
            total += jnp.where(parent_ref[t, s] == SLOTS * leaf + p, placed[s], 0.0)
        kept[p] = total

    def sort_inbox(t):
        swap(t).wait()
        for s in range(SLOTS):
            values = inbox[t, s].astype(F32)
            parent = guest[t, s:s + 1, ROWS:]
            for p in range(SLOTS):
                mine = jnp.where(parent == SLOTS * leaf + p, values, 0.0)
                sorted_in[p * COLS:(p + 1) * COLS, s * ROWS:(s + 1) * ROWS] = mine.astype(BF16)

    def land(t, half):
        columns = slice(half * 256, half * 256 + 256)
        result = lax.dot_general(sorted_in[...], guest_marks[t, columns], NT, preferred_element_type=F32)
        for p in range(SLOTS):
            kept[p, :, columns] += result[p * COLS:(p + 1) * COLS]

    plan = {}

    def at(slot, unit):
        plan.setdefault(slot, []).append(unit)

    start = {(t, piece): first for t, piece, first in PIECES}
    def first_at(slot):
        return min(i for i, (_, piece, first) in enumerate(PIECES) if first <= slot <= first + REACH[piece])

    for t in range(TIERS):
        early = min(start[t, 0], start[t, 1]) - 2
        if early < 0:
            pack(t)
        else:
            at((early, first_at(early)), functools.partial(pack, t))
        if start[t, 2] < 1:
            loads[2 * t + 1].wait()
        else:
            at((start[t, 2] - 1, first_at(start[t, 2] - 1)), loads[2 * t + 1].wait)
    for t in range(TIERS - 1):
        describe(t)
    pl.semaphore_wait(barrier, 2 + TIERS - 1)
    for t in range(TIERS - 1):
        introduce(t).start()

    places = [
        (slot, i)
        for slot in range(LAST + 1)
        for i, (_, piece, first) in enumerate(PIECES)
        if first <= slot <= first + REACH[piece]
    ]
    rank = {(t, piece): i for i, (t, piece, _) in enumerate(PIECES)}
    here = 0

    def complete(t, *pieces):
        return max((start[t, piece] + REACH[piece], rank[t, piece]) for piece in pieces)

    def enqueue(unit, earliest=(0, 0), apart=1):
        nonlocal here
        while here < len(places) and places[here] < earliest:
            here += 1
        spot = places[here] if here < len(places) else (LAST + 1, 0)
        at(spot, unit)
        here += apart
        return spot

    for t in range(TIERS - 1):
        at(places[4 + 8 * t], introduce(t).wait)
        for s in range(SLOTS):
            at(places[4 + 8 * t + 2 * s], functools.partial(mark, rows_ref, marks, t, s))
            at(places[5 + 8 * t + 2 * s], functools.partial(mark, guest, guest_marks, t, s))
    sent = (0, 0)
    for t in range(TIERS):
        earliest = complete(t, 0, 1)
        if t:
            arrival = (sent[0] + SWAP_SLOTS[t - 1], sent[1])
            enqueue(functools.partial(sort_inbox, t - 1), arrival)
            enqueue(functools.partial(land, t - 1, 0))
            enqueue(functools.partial(land, t - 1, 1))
        for s in range(SLOTS):
            enqueue(functools.partial(make_source, t, s), earliest)
        for half, part in ((0, 0), (1, 0), (1, 1)):
            enqueue(functools.partial(solve, t, half, part))
        if t < TIERS - 1:
            earliest = complete(t, 2)
            for s in range(SLOTS):
                enqueue(functools.partial(update, t, s), earliest)
            sent = enqueue(lambda t=t: swap(t).start())
            for s in range(SLOTS):
                enqueue(functools.partial(place, t, s))
            for p in range(SLOTS):
                enqueue(functools.partial(collect, t, p))

    def serve(slot, receiving):
        for i, (t, piece, first) in enumerate(PIECES):
            k = slot - first
            if receiving:
                @pl.when(jnp.logical_and(k >= 0, k <= REACH[piece]))
                def _():
                    for direction in range(2):
                        gather(direction, piece, t, k)
                    for when, units in plan.items():
                        if when[1] == i and when[0] <= LAST:
                            @pl.when(slot == when[0])
                            def _():
                                for unit in units:
                                    unit()

        for t, piece, first in PIECES:
            k = slot - first - LAG

            @pl.when(jnp.logical_and(k >= 0, k < REACH[piece]))
            def _():
                for direction in range(2):
                    drain(direction, piece, t, k)

    def step(slot, carry):
        serve(slot, True)
        return carry

    lax.fori_loop(0, LAST + 1, step, 0)
    for when in sorted(plan):
        if when[0] > LAST:
            for unit in plan[when]:
                unit()
    for s in range(SLOTS):
        top[s] = updated(TIERS - 1, s).astype(BF16)
    last = pltpu.make_async_copy(top, upward_hbm, store_sem.at[TIERS])
    last.start()

    def finish(slot, carry):
        serve(slot, False)
        return carry

    lax.fori_loop(LAST + 1, LAST + LAG, finish, 0)
    for t in range(TIERS):
        store(t).wait()
    last.wait()


def on_device(histograms, diag_inv, below_panel, parent_map, row_lists):
    vmem = pltpu.VMEM
    dma = pltpu.SemaphoreType.DMA
    return pl.pallas_call(
        kernel,
        out_shape=(
            jax.ShapeDtypeStruct((TIERS, SLOTS, COLS, WIDTH), BF16),
            jax.ShapeDtypeStruct((SLOTS, COLS, ROWS), BF16),
        ),
        in_specs=[
            pl.BlockSpec(memory_space=pl.ANY),
            pl.BlockSpec(memory_space=pl.ANY),
            pl.BlockSpec(memory_space=pl.ANY),
            pl.BlockSpec(memory_space=pltpu.SMEM),
            pl.BlockSpec(memory_space=pltpu.VMEM),
        ],
        out_specs=(pl.BlockSpec(memory_space=pl.ANY), pl.BlockSpec(memory_space=pl.ANY)),
        scratch_shapes=[
            vmem((TIERS, SLOTS, COLS, WIDTH), BF16),
            vmem((TIERS, SLOTS, PIECE, WIDTH), BF16),
            vmem((TIERS, RING, RING, PIECE, LANES), BF16),
            vmem((TIERS, RING, SLOTS, DEPTH, WIDTH), BF16),
            vmem((SLOTS * COLS, RING * LANES), BF16),
            vmem((TIERS, SLOTS, COLS, WIDTH), BF16),
            vmem((SLOTS, COLS, WIDTH), F32),
            vmem((SLOTS, COLS, WIDTH), F32),
            vmem((SLOTS * COLS, 256), F32),
            vmem((SLOTS, COLS, ROWS), BF16),
            vmem((TIERS - 1, WIDTH, SLOTS * ROWS), BF16),
            vmem((TIERS - 1, WIDTH, SLOTS * ROWS), BF16),
            vmem((TIERS - 1, SLOTS, 2 * ROWS), jnp.int32),
            vmem((TIERS - 1, SLOTS, 2 * ROWS), jnp.int32),
            vmem((SLOTS * COLS, SLOTS * ROWS), BF16),
            vmem((TIERS - 1, SLOTS, COLS, ROWS), BF16),
            vmem((TIERS - 1, SLOTS, COLS, ROWS), BF16),
            vmem((SLOTS, COLS, ROWS), BF16),
            dma((2 * TIERS + 1,)),
            dma((2, 3, TIERS, MAX_HOP + 1)),
            dma((2, 3, TIERS, MAX_HOP + 1)),
            dma((TIERS - 1,)),
            dma((TIERS - 1,)),
            dma((TIERS - 1,)),
            dma((TIERS - 1,)),
            dma((TIERS + 1,)),
        ],
        compiler_params=pltpu.CompilerParams(
            collective_id=0, has_side_effects=True, vmem_limit_bytes=60 << 20
        ),
    )(histograms, diag_inv, below_panel, parent_map, row_lists)


def solution(mesh):
    return jax.shard_map(
        on_device,
        mesh=mesh,
        in_specs=(
            P(None, "leaf", "col", None),
            P(None, "leaf", "col", None),
            P(None, "leaf", "col", None),
            P(None, "leaf"),
            P(None, "leaf", None),
        ),
        out_specs=(P(None, "leaf", "col", None), P("leaf", "col", None)),
        check_vma=False,
    )
```

```python
import functools
import jax
import jax.numpy as jnp
from jax import lax
from jax.experimental import pallas as pl
from jax.experimental.pallas import tpu as pltpu
from jax.sharding import PartitionSpec as P

MESH = pl.DeviceIdType.MESH
F32, BF16 = jnp.float32, jnp.bfloat16

RING = 16
TIERS = 4
SLOTS = 4
COLS = 64
WIDTH = 512
ROWS = 256
PIECE = 32
DEPTH = 16
LANES = 128
NARROW = 32

HOPS_UP = (
    (9, 8, 6, 7, 7, 6, 6, 7, 6, 6, 7, 9, 9, 6, 9, 9),
    (9, 8, 10, 9, 6, 5, 8, 9, 7, 7, 8, 8, 8, 7, 8, 8),
    (10, 10, 10, 6, 9, 8, 6, 6, 6, 6, 5, 5, 10, 8, 10, 10),
)
PIECES = (
    (0, 0, 0),
    (1, 2, 0),
    (0, 1, 1),
    (2, 1, 7),
    (3, 2, 10),
    (3, 1, 11),
    (2, 2, 5),
    (1, 1, 4),
    (0, 2, 0),
    (3, 0, 9),
    (2, 0, 5),
    (1, 0, 2),
)
MAX_HOP = 10
REACH = tuple(
    max(max(r, 15 - r) for r in (up[8:] if piece == 1 else up)) for piece, up in enumerate(HOPS_UP)
)
LAG = 6
PHASES = 3
LAST = max(start + REACH[piece] for _, piece, start in PIECES)
HALF = RING // 2
SWAP_SLOTS = (1, 2, 2)
NT = (((1,), (1,)), ((), ()))


def table(values):
    low = sum((v - 5) << (3 * i) for i, v in enumerate(values[:8]))
    high = sum((v - 5) << (3 * i) for i, v in enumerate(values[8:]))
    return low, high


def hops_up(words, z):
    word = jnp.where(z < 8, jnp.int32(words[0]), jnp.int32(words[1]))
    return 5 + lax.rem(lax.shift_right_logical(word, 3 * lax.rem(z, 8)), 8)


def by_width(w, act, low=0, high=HALF):
    if high - low == 1:
        act(high)
        return
    middle = (low + high) // 2

    def lower():
        by_width(w, act, low, middle)

    def upper():
        by_width(w, act, middle, high)

    lax.cond(w < middle, lower, upper)


def kernel(
    hist_hbm, diag_hbm, below_hbm, parent_ref, rows_ref,
    solved_hbm, upward_hbm,
    hist, diag, gathered, panels, spread, answer, kept, placed, partial, lower, marks, guest_marks, card, guest, sorted_in, outbox, inbox, top,
    load_sem, ring_send, ring_recv, swap_send, swap_recv, card_send, card_recv, store_sem,
):
    me = lax.axis_index("col")
    leaf = lax.axis_index("leaf")
    above = lax.rem(me + 1, RING)
    under = lax.rem(me + RING - 1, RING)
    ups = [table(values) for values in HOPS_UP]

    def partner(bit):
        return leaf + (1 << bit) * (1 - 2 * lax.rem(leaf // (1 << bit), 2))

    loads = [
        pltpu.make_async_copy(diag_hbm.at[0], diag.at[0], load_sem.at[0]),
        pltpu.make_async_copy(below_hbm.at[0], panels.at[0, me], load_sem.at[1]),
    ]
    for t in range(1, TIERS):
        loads.append(pltpu.make_async_copy(diag_hbm.at[t], diag.at[t], load_sem.at[2 * t]))
        loads.append(pltpu.make_async_copy(below_hbm.at[t], panels.at[t, me], load_sem.at[2 * t + 1]))
    loads.append(pltpu.make_async_copy(hist_hbm, hist, load_sem.at[2 * TIERS]))
    for load in loads:
        load.start()

    barrier = pltpu.get_barrier_semaphore()
    for ring in (above, under):
        pl.semaphore_signal(barrier, inc=1, device_id={"col": ring}, device_id_type=MESH)
    for bit in range(TIERS - 1):
        pl.semaphore_signal(barrier, inc=1, device_id={"leaf": partner(bit)}, device_id_type=MESH)

    group = lax.broadcasted_iota(jnp.int32, (1, LANES), 1) // NARROW

    def pack(t):
        loads[2 * t].wait()
        for q in range(WIDTH // LANES):
            wide = [diag[t, s, :, q * LANES:(q + 1) * LANES].astype(F32) for s in range(SLOTS)]
            for a in range(LANES // NARROW):
                tile = jnp.zeros((PIECE, LANES), F32)
                for s in range(SLOTS):
                    turn = NARROW * ((s - a) % 4)
                    moved = pltpu.roll(wide[s], turn, axis=1) if turn else wide[s]
                    tile = jnp.where(group == s, moved, tile)
                gathered[t, me, 4 * q + a] = tile.astype(BF16)

    def aim(direction, piece, k):
        z = lax.rem(me - k + RING, RING) if direction == 0 else lax.rem(me + k, RING)
        far = hops_up(ups[piece], z)
        if direction:
            far = RING - 1 - far
        if piece == 1:
            far = jnp.where(z >= HALF, far, -1)
        return z, far

    def each_block(piece, t, z, act):
        if piece == 2:
            act(panels.at[t, z])
        elif piece == 1:
            by_width(z - HALF, lambda n: act(gathered.at[t, z, pl.ds(HALF, n)]))
        else:
            by_width(jnp.minimum(z, HALF - 1), lambda n: act(gathered.at[t, z, pl.ds(0, n)]))

    def ring_copy(direction, piece, t, block, k, landed):
        return pltpu.make_async_remote_copy(
            src_ref=block, dst_ref=block,
            send_sem=ring_send.at[direction, piece, t, k],
            recv_sem=ring_recv.at[direction, piece, t, landed],
            device_id={"col": above if direction == 0 else under}, device_id_type=MESH,
        )

    def gather(direction, piece, t, k):
        z, far = aim(direction, piece, k)

        def act(block):
            @pl.when(k >= 1)
            def _():
                ring_copy(direction, piece, t, block, k, jnp.maximum(k - 1, 0)).wait_recv()

            @pl.when(k < far)
            def _():
                ring_copy(direction, piece, t, block, k, k).start()

        @pl.when(k <= far)
        def _():
            each_block(piece, t, z, act)

    def drain(direction, piece, t, k):
        z, far = aim(direction, piece, k)

        @pl.when(k < far)
        def _():
            each_block(piece, t, z, lambda block: ring_copy(direction, piece, t, block, k, k).wait_send())

    def swap(t):
        return pltpu.make_async_remote_copy(
            src_ref=outbox.at[t], dst_ref=inbox.at[t],
            send_sem=swap_send.at[t], recv_sem=swap_recv.at[t],
            device_id={"leaf": partner(t)}, device_id_type=MESH,
        )

    def store(t):
        return pltpu.make_async_copy(answer.at[t], solved_hbm.at[t], store_sem.at[t])

    def make_source(t, s):
        if s == 0:
            if t == 0:
                loads[2 * TIERS].wait()
        values = hist[t, s].astype(F32)
        if t > 0:
            values = values - kept[s]
        values = values.astype(BF16).astype(F32)
        for m in range(WIDTH // NARROW):
            q, a = m // 4, m % 4
            tile = values[:, q * LANES:(q + 1) * LANES]
            turn = NARROW * ((s - a) % 4)
            if turn:
                tile = pltpu.roll(tile, turn, axis=1)
            tile = jnp.where(group == s, tile, 0.0).astype(BF16)
            spread[s * COLS:(s + 1) * COLS, m * LANES:(m + 1) * LANES] = tile

    def solve(t, half, part):
        columns = []
        for m in range(HALF * part, HALF * part + HALF):
            blocks = []
            for z in range(HALF * half, HALF * half + HALF):
                blocks.append(gathered[t, z, m] if z >= m else jnp.zeros((PIECE, LANES), BF16))
            columns.append(jnp.concatenate(blocks, axis=0))
        weights = jnp.concatenate(columns, axis=1)
        result = lax.dot_general(
            spread[:, HALF * LANES * part:HALF * LANES * (part + 1)], weights, NT, preferred_element_type=F32
        )
        if half == 1 and part == 0:
            partial[...] = result
            return
        if half == 1:
            result = partial[...] + result
        result = result.astype(BF16)
        for s in range(SLOTS):
            answer[t, s, :, half * 256:(half + 1) * 256] = result[s * COLS:(s + 1) * COLS]
        if half == 1:
            store(t).start()

    def updated(t, s):
        panel = jnp.concatenate([panels[t, z, s] for z in range(RING)], axis=0)
        return lax.dot_general(answer[t, s], panel, NT, preferred_element_type=F32)

    def mark(source, marks, t, s):
        hit = lax.broadcasted_iota(jnp.int32, (WIDTH, ROWS), 0) == source[t, s:s + 1, :ROWS]
        marks[t, :, s * ROWS:(s + 1) * ROWS] = hit.astype(F32).astype(BF16)

    def describe(t):
        card[t, :, :ROWS] = rows_ref[t]
        for s in range(SLOTS):
            card[t, s:s + 1, ROWS:] = jnp.full((1, ROWS), parent_ref[t, s], jnp.int32)

    def introduce(t):
        return pltpu.make_async_remote_copy(
            src_ref=card.at[t], dst_ref=guest.at[t],
            send_sem=card_send.at[t], recv_sem=card_recv.at[t],
            device_id={"leaf": partner(t)}, device_id_type=MESH,
        )

    def update(t, s):
        value = updated(t, s)
        upper = value.astype(BF16)
        outbox[t, s] = upper
        lower[s] = (value - upper.astype(F32)).astype(BF16)

    def place(t, s):
        both = jnp.concatenate([outbox[t, s], lower[s]], axis=0)
        result = lax.dot_general(both, marks[t, :, s * ROWS:(s + 1) * ROWS], NT, preferred_element_type=F32)
        placed[s] = result[:COLS] + result[COLS:]

    def collect(t, p):
        total = jnp.zeros((COLS, WIDTH), F32)
        for s in range(SLOTS):
            total += jnp.where(parent_ref[t, s] == SLOTS * leaf + p, placed[s], 0.0)
        kept[p] = total

    def sort_inbox(t):
        swap(t).wait()
        for s in range(SLOTS):
            values = inbox[t, s].astype(F32)
            parent = guest[t, s:s + 1, ROWS:]
            for p in range(SLOTS):
                mine = jnp.where(parent == SLOTS * leaf + p, values, 0.0)
                sorted_in[p * COLS:(p + 1) * COLS, s * ROWS:(s + 1) * ROWS] = mine.astype(BF16)

    def land(t, half):
        columns = slice(half * 256, half * 256 + 256)
        result = lax.dot_general(sorted_in[...], guest_marks[t, columns], NT, preferred_element_type=F32)
        for p in range(SLOTS):
            kept[p, :, columns] += result[p * COLS:(p + 1) * COLS]

    plan = {}

    def at(slot, unit):
        plan.setdefault(slot, []).append(unit)

    start = {(t, piece): first for t, piece, first in PIECES}
    def first_at(slot):
        return min(i for i, (_, piece, first) in enumerate(PIECES) if first <= slot <= first + REACH[piece])

    for t in range(TIERS):
        early = min(start[t, 0], start[t, 1]) - 2
        if early < 0:
            pack(t)
        else:
            at((early, first_at(early)), functools.partial(pack, t))
        if start[t, 2] < 1:
            loads[2 * t + 1].wait()
        else:
            at((start[t, 2] - 1, first_at(start[t, 2] - 1)), loads[2 * t + 1].wait)
    for t in range(TIERS - 1):
        describe(t)
    pl.semaphore_wait(barrier, 2 + TIERS - 1)
    for t in range(TIERS - 1):
        introduce(t).start()

    places = [
        (slot, i)
        for slot in range(LAST + 1)
        for i, (_, piece, first) in enumerate(PIECES)
        if first <= slot <= first + REACH[piece]
    ]
    rank = {(t, piece): i for i, (t, piece, _) in enumerate(PIECES)}
    here = 0

    def complete(t, *pieces):
        return max((start[t, piece] + REACH[piece], rank[t, piece]) for piece in pieces)

    def enqueue(unit, earliest=(0, 0), apart=1):
        nonlocal here
        while here < len(places) and places[here] < earliest:
            here += 1
        spot = places[here] if here < len(places) else (LAST + 1, 0)
        at(spot, unit)
        here += apart
        return spot

    for t in range(TIERS - 1):
        at(places[4 + 8 * t], introduce(t).wait)
        for s in range(SLOTS):
            at(places[4 + 8 * t + 2 * s], functools.partial(mark, rows_ref, marks, t, s))
            at(places[5 + 8 * t + 2 * s], functools.partial(mark, guest, guest_marks, t, s))
    sent = (0, 0)
    for t in range(TIERS):
        if t:
            arrival = (sent[0] + SWAP_SLOTS[t - 1], sent[1])
            enqueue(functools.partial(sort_inbox, t - 1), arrival)
            enqueue(functools.partial(land, t - 1, 0))
            enqueue(functools.partial(land, t - 1, 1))
        for s in range(SLOTS):
            enqueue(functools.partial(make_source, t, s))
        enqueue(functools.partial(solve, t, 0, 0), complete(t, 0))
        enqueue(functools.partial(solve, t, 1, 0))
        enqueue(functools.partial(solve, t, 1, 1), complete(t, 1))
        if t < TIERS - 1:
            earliest = complete(t, 2)
            for s in range(SLOTS):
                enqueue(functools.partial(update, t, s), earliest)
            sent = enqueue(lambda t=t: swap(t).start())
            for s in range(SLOTS):
                enqueue(functools.partial(place, t, s))
            for p in range(SLOTS):
                enqueue(functools.partial(collect, t, p))

    def serve(slot, receiving, low, high):
        for i, (t, piece, first) in enumerate(PIECES):
            k = slot - first
            if receiving and first < high and first + REACH[piece] >= low:
                @pl.when(jnp.logical_and(k >= 0, k <= REACH[piece]))
                def _():
                    for direction in range(2):
                        gather(direction, piece, t, k)
                    for when, units in plan.items():
                        if when[1] == i and low <= when[0] < high:
                            @pl.when(slot == when[0])
                            def _():
                                for unit in units:
                                    unit()

        for t, piece, first in PIECES:
            if first + LAG >= high or first + LAG + REACH[piece] <= low:
                continue
            k = slot - first - LAG

            @pl.when(jnp.logical_and(k >= 0, k < REACH[piece]))
            def _():
                for direction in range(2):
                    drain(direction, piece, t, k)

    cuts = [(LAST + 1) * i // PHASES for i in range(PHASES + 1)]
    for low, high in zip(cuts[:-1], cuts[1:]):
        def step(slot, carry, low=low, high=high):
            serve(slot, True, low, high)
            return carry

        lax.fori_loop(low, high, step, 0)
    for when in sorted(plan):
        if when[0] > LAST:
            for unit in plan[when]:
                unit()
    for s in range(SLOTS):
        top[s] = updated(TIERS - 1, s).astype(BF16)
    last = pltpu.make_async_copy(top, upward_hbm, store_sem.at[TIERS])
    last.start()

    def finish(slot, carry):
        serve(slot, False, LAST + 1, LAST + LAG)
        return carry

    lax.fori_loop(LAST + 1, LAST + LAG, finish, 0)
    for t in range(TIERS):
        store(t).wait()
    last.wait()


def on_device(histograms, diag_inv, below_panel, parent_map, row_lists):
    vmem = pltpu.VMEM
    dma = pltpu.SemaphoreType.DMA
    return pl.pallas_call(
        kernel,
        out_shape=(
            jax.ShapeDtypeStruct((TIERS, SLOTS, COLS, WIDTH), BF16),
            jax.ShapeDtypeStruct((SLOTS, COLS, ROWS), BF16),
        ),
        in_specs=[
            pl.BlockSpec(memory_space=pl.ANY),
            pl.BlockSpec(memory_space=pl.ANY),
            pl.BlockSpec(memory_space=pl.ANY),
            pl.BlockSpec(memory_space=pltpu.SMEM),
            pl.BlockSpec(memory_space=pltpu.VMEM),
        ],
        out_specs=(pl.BlockSpec(memory_space=pl.ANY), pl.BlockSpec(memory_space=pl.ANY)),
        scratch_shapes=[
            vmem((TIERS, SLOTS, COLS, WIDTH), BF16),
            vmem((TIERS, SLOTS, PIECE, WIDTH), BF16),
            vmem((TIERS, RING, RING, PIECE, LANES), BF16),
            vmem((TIERS, RING, SLOTS, DEPTH, WIDTH), BF16),
            vmem((SLOTS * COLS, RING * LANES), BF16),
            vmem((TIERS, SLOTS, COLS, WIDTH), BF16),
            vmem((SLOTS, COLS, WIDTH), F32),
            vmem((SLOTS, COLS, WIDTH), F32),
            vmem((SLOTS * COLS, 256), F32),
            vmem((SLOTS, COLS, ROWS), BF16),
            vmem((TIERS - 1, WIDTH, SLOTS * ROWS), BF16),
            vmem((TIERS - 1, WIDTH, SLOTS * ROWS), BF16),
            vmem((TIERS - 1, SLOTS, 2 * ROWS), jnp.int32),
            vmem((TIERS - 1, SLOTS, 2 * ROWS), jnp.int32),
            vmem((SLOTS * COLS, SLOTS * ROWS), BF16),
            vmem((TIERS - 1, SLOTS, COLS, ROWS), BF16),
            vmem((TIERS - 1, SLOTS, COLS, ROWS), BF16),
            vmem((SLOTS, COLS, ROWS), BF16),
            dma((2 * TIERS + 1,)),
            dma((2, 3, TIERS, MAX_HOP + 1)),
            dma((2, 3, TIERS, MAX_HOP + 1)),
            dma((TIERS - 1,)),
            dma((TIERS - 1,)),
            dma((TIERS - 1,)),
            dma((TIERS - 1,)),
            dma((TIERS + 1,)),
        ],
        compiler_params=pltpu.CompilerParams(
            collective_id=0, has_side_effects=True, vmem_limit_bytes=60 << 20
        ),
    )(histograms, diag_inv, below_panel, parent_map, row_lists)


def solution(mesh):
    return jax.shard_map(
        on_device,
        mesh=mesh,
        in_specs=(
            P(None, "leaf", "col", None),
            P(None, "leaf", "col", None),
            P(None, "leaf", "col", None),
            P(None, "leaf"),
            P(None, "leaf", None),
        ),
        out_specs=(P(None, "leaf", "col", None), P("leaf", "col", None)),
        check_vma=False,
    )
```
